32 devices in a mesh: depth: 16 (over z, x, core), tile: 2 (over y).
Axes of the slice: x: 2, y: 2, z: 4, core: 2. Of those that a mesh axis runs over, the one named last changes fastest.
Arguments:
- density: bfloat16 [3, 128, 4, 4096], P(None, 'depth', 'tile'), may hold values from 0 to 1
- material_weight: float32 [4, 3], replicated, may hold values from 0.3 to 3
- color_table: int32 [4, 4, 256], replicated, may hold values from 0 to 255
Outputs:
- pixels: float32 [4, 4, 4, 4096], P(None, None, 'tile', 'depth')
The draws below stay inside these ranges and needn't reach their ends.
Inputs may be any that keep to these rules, and one draw needn't show every extreme that they name: `color_table`: levels of a transfer function, 255 meaning full.
All inputs are finite; a program needn't handle non-finite values.
Results may differ from the reference program's by a relative error of at most 0.0003.
Values may be sent and summed in bfloat16 or wider, within the bound.
A program may use at most 128 MiB of HBM per device.

```python
import math
import jax
import jax.numpy as jnp
from jax import lax

MATS = 3
ENERGIES = 4
BINS = 256
NX = 4096
NZ = 128
NY = 4


def touch_ends(values, rng, low, high):
    spot = [jax.random.randint(jax.random.fold_in(rng, axis), (), 0, length) for axis, length in enumerate(values.shape)]
    main_axis = values.shape.index(max(values.shape))
    next_to = spot[:main_axis] + [(spot[main_axis] + 1) % values.shape[main_axis]] + spot[main_axis + 1:]
    return values.at[tuple(spot)].set(low).at[tuple(next_to)].set(high)


def block_levels(rng, dims, pieces, smallest, high):
    level = 1.0
    for dim, shards_of in pieces:
        steps = jax.random.uniform(jax.random.fold_in(jax.random.fold_in(rng, 6), dim), (shards_of,), jnp.float32, smallest / len(pieces), high / len(pieces))
        level = level * jnp.repeat(jnp.exp(steps), dims[dim] // shards_of).reshape((-1,) + (1,) * (len(dims) - 1 - dim))
    return level


def setup_inputs(seed: int = 0) -> dict:
    arg_keys = jax.random.split(jax.random.key(seed), 4)
    return {
        "density": jnp.clip(1.0 * jax.random.uniform(arg_keys[0], (MATS, NZ, NY, NX), jnp.float32) ** block_levels(arg_keys[0], (MATS, NZ, NY, NX), ((1, 16), (2, 2)), -0.2, 0.2), 0.0, 1.0).astype(jnp.bfloat16),
        "material_weight": jnp.clip(jnp.exp(jax.random.uniform(arg_keys[1], (ENERGIES, MATS), jnp.float32, math.log(0.3), math.log(3.0))), 0.3, 3.0),
        "color_table": touch_ends(jax.random.randint(arg_keys[2], (ENERGIES, 4, BINS), 0, 256), jax.random.fold_in(arg_keys[2], 1), 0, 255).astype(jnp.int32),
    }


def shade_samples(middle, slope_z, slope_y, slope_x, material_weight, color_table, depth_total):
    highest = lax.Precision.HIGHEST
    atten = jnp.dot(material_weight, middle, precision=highest)
    grad_z = jnp.dot(material_weight, slope_z, precision=highest)
    grad_y = jnp.dot(material_weight, slope_y, precision=highest)
    grad_x = jnp.dot(material_weight, slope_x, precision=highest)
    slope_sq = grad_z * grad_z + grad_y * grad_y + grad_x * grad_x
    shading = 0.3 + 0.7 * jnp.abs(0.8 * grad_z + 0.48 * grad_y + 0.36 * grad_x) / jnp.sqrt(slope_sq + 1.0)
    gate_term = slope_sq / (1.0 + slope_sq)
    table_level = 255.0 * (1.0 - jnp.exp(-0.5 * atten))
    bin_centers = jnp.arange(color_table.shape[2], dtype=jnp.float32)[:, None]
    looked = []
    for energy in range(material_weight.shape[0]):
        hat_weights = jnp.maximum(0.0, 1.0 - jnp.abs(table_level[energy][None, :] - bin_centers)).astype(jnp.bfloat16)
        looked.append(jnp.dot(color_table[energy].astype(jnp.bfloat16), hat_weights, preferred_element_type=jnp.float32))
    colour = jnp.stack(looked) / 255.0
    opacity = colour[:, 3] * gate_term * (6.0 / depth_total)
    emission = opacity[:, None] * colour[:, :3] * shading[:, None]
    return (emission, 1.0 - opacity)

def reference(density, material_weight, color_table):
    mats, planes, height, columns = density.shape
    energies = material_weight.shape[0]
    padded = jnp.pad(density, ((0, 0), (1, 1), (1, 1), (1, 1)))

    def per_row(index):
        window = lax.dynamic_slice_in_dim(padded, index, 3, 2).astype(jnp.float32)
        middle = window[:, 1:-1, 1, 1:-1].reshape(mats, planes * columns)
        slope_z = ((window[:, 2:, 1, 1:-1] - window[:, :-2, 1, 1:-1]) * 0.5).reshape(mats, planes * columns)
        slope_y = ((window[:, 1:-1, 2, 1:-1] - window[:, 1:-1, 0, 1:-1]) * 0.5).reshape(mats, planes * columns)
        slope_x = ((window[:, 1:-1, 1, 2:] - window[:, 1:-1, 1, :-2]) * 0.5).reshape(mats, planes * columns)
        emission, transmit = shade_samples(middle, slope_z, slope_y, slope_x, material_weight, color_table, planes)
        emission = emission.reshape(energies, 3, planes, columns)
        transmit = transmit.reshape(energies, planes, columns)
        inclusive = jnp.cumprod(transmit, axis=1)
        exclusive = jnp.concatenate([jnp.ones_like(inclusive[:, :1]), inclusive[:, :-1]], axis=1)
        colour = lax.optimization_barrier(jnp.sum(exclusive[:, None] * emission, axis=2))
        return jnp.concatenate([colour, (1.0 - inclusive[:, -1])[:, None]], axis=1)
    result = lax.map(per_row, jnp.arange(height, dtype=jnp.int32))
    return result.transpose(1, 2, 0, 3)
```

```python
import functools

import jax
import jax.numpy as jnp
from jax import lax
from jax.experimental import pallas as pl
from jax.experimental.pallas import tpu as pltpu
from jax.sharding import PartitionSpec as P

LANES = 128
SUB = 8


def pack_tables(table_ref, tabs):
    for e in range(table_ref.shape[0]):
        word = (
            table_ref[e, 0:1, :]
            + table_ref[e, 1:2, :] * 256
            + table_ref[e, 2:3, :] * 65536
            + lax.shift_left(table_ref[e, 3:4, :], 24)
        )
        bins = word.shape[1]
        pair = (word, pltpu.roll(word, bins - 1, 1))
        for k in range(2):
            for half in range(bins // LANES):
                tabs[e, k, half] = jnp.broadcast_to(
                    pair[k][:, half * LANES : (half + 1) * LANES], (SUB, LANES)
                )


def look_up(tabs, e, k, idx, where_half):
    found = None
    for half in range(tabs.shape[2]):
        piece = jnp.take_along_axis(tabs[e, k, half], idx, axis=1, mode="promise_in_bounds")
        found = piece if found is None else jnp.where(where_half == half, piece, found)
    return found


def channels_of(word):
    return (
        (word & 255).astype(jnp.float32),
        (lax.shift_right_logical(word, 8) & 255).astype(jnp.float32),
        (lax.shift_right_logical(word, 16) & 255).astype(jnp.float32),
        lax.shift_right_logical(word, 24).astype(jnp.float32),
    )


def mixer(weight_ref, e):
    w = [weight_ref[e, m] for m in range(weight_ref.shape[1])]

    def mix(values):
        total = w[0] * values[0]
        for m in range(1, len(values)):
            total = total + w[m] * values[m]
        return total

    return mix


def tile_levels(grid_ref, tabs, weight_ref, levels, y, tile, scale):
    mats, planes = grid_ref.shape[:2]
    for z in range(planes):
        mid = [grid_ref[m, z, y, tile].astype(jnp.float32) for m in range(mats)]
        for e in range(weight_ref.shape[0]):
            atten = mixer(weight_ref, e)(mid)
            level = 255.0 - 255.0 * jnp.exp(-0.5 * atten)
            bin_at = level.astype(jnp.int32)
            frac = level - bin_at.astype(jnp.float32)
            w1 = frac.astype(jnp.bfloat16).astype(jnp.float32)
            w0 = (1.0 - frac).astype(jnp.bfloat16).astype(jnp.float32)
            idx = bin_at & (LANES - 1)
            half = lax.shift_right_logical(bin_at, 7)
            low = channels_of(look_up(tabs, e, 0, idx, half))
            high = channels_of(look_up(tabs, e, 1, idx, half))
            for c in range(4):
                value = w0 * low[c] + w1 * high[c]
                levels[y, tile, z, e * 4 + c] = value * scale if c == 3 else value


def tile_image(dens, levels, weight_ref, y, tile, planes):
    mats = dens.shape[0]
    energies = weight_ref.shape[0]
    lane = lax.broadcasted_iota(jnp.int32, (SUB, LANES), 1)
    first, last = lane == 0, lane == LANES - 1
    base = tile * SUB + SUB
    rows = pl.ds(pl.multiple_of(base, SUB), SUB)
    ahead = [None] * energies
    sums = [[None] * 3 for _ in range(energies)]
    for z in range(planes):
        dz, dy, dx = [], [], []
        for m in range(mats):
            here = dens[m, z + 1, y + 1, rows, :]
            dz.append(dens[m, z + 2, y + 1, rows, :] - dens[m, z, y + 1, rows, :])
            dy.append(dens[m, z + 1, y + 2, rows, :] - dens[m, z + 1, y, rows, :])
            above = dens[m, z + 1, y + 1, pl.ds(base - 1, SUB), :]
            below = dens[m, z + 1, y + 1, pl.ds(base + 1, SUB), :]
            right = pltpu.roll(jnp.where(first, below, here), LANES - 1, 1)
            left = pltpu.roll(jnp.where(last, above, here), 1, 1)
            dx.append(right - left)
        for e in range(energies):
            mix = mixer(weight_ref, e)
            gz, gy, gx = mix(dz) * 0.5, mix(dy) * 0.5, mix(dx) * 0.5
            sq = gz * gz + gy * gy + gx * gx
            inv = lax.rsqrt(sq + 1.0)
            shading = 0.3 + 0.7 * jnp.abs(0.8 * gz + 0.48 * gy + 0.36 * gx) * inv
            opacity = levels[y, tile, z, e * 4 + 3] * (sq * inv * inv)
            lit = opacity * shading
            if z:
                lit = lit * ahead[e]
            for c in range(3):
                term = lit * levels[y, tile, z, e * 4 + c]
                sums[e][c] = term if z == 0 else sums[e][c] + term
            transmit = 1.0 - opacity
            ahead[e] = transmit if z == 0 else ahead[e] * transmit
    return sums, ahead


def far_first(mine, step, tiles):
    if tiles & (tiles - 1):
        return (mine + 1 + step) % tiles
    other, result, bit = tiles - 1 - step, 0, 1
    while bit < tiles:
        result = result + bit * ((mine // bit + other // bit) % 2)
        bit *= 2
    return result


def render_kernel(
    depth_total, mixed_ref, table_ref, weight_ref, out_ref,
    grid_ref, wide, dens, tabs, levels, z_in, y_in, image, pair_in, got,
    z_send, z_recv, y_send, y_recv, pair_send, pair_recv, send_sem, recv_sem,
):
    mats, planes, lines, tiles = grid_ref.shape[:4]
    strips = tiles * SUB
    energies = weight_ref.shape[0]
    pairs, block, _ = got.shape
    count = 2 * pairs
    per_tile = count // tiles
    half_tile = per_tile // 2
    group = energies * lines
    stride = 4 * group
    me, row = lax.axis_index("depth"), lax.axis_index("tile")
    rows_of = lax.axis_size("tile")
    has_z = (me > 0, me < count - 1)
    has_y = (row > 0, row < rows_of - 1)
    z_peer = (me - 1, me + 1)
    y_peer = (row - 1, row + 1)
    mine = me // per_tile
    core, pair = me % 2, me // 2
    partner = me + 1 - 2 * core

    barrier = pltpu.get_barrier_semaphore()

    def greet(o, carry):
        @pl.when(o != pair)
        def _():
            pl.semaphore_signal(
                barrier, inc=1, device_id={"depth": 2 * o + core},
                device_id_type=pl.DeviceIdType.MESH,
            )
        return carry

    for side in range(2):
        @pl.when(has_y[side])
        def _():
            pl.semaphore_signal(
                barrier, inc=1, device_id={"tile": y_peer[side]},
                device_id_type=pl.DeviceIdType.MESH,
            )

        @pl.when(has_z[side])
        def _():
            pl.semaphore_signal(
                barrier, inc=1, device_id={"depth": z_peer[side]},
                device_id_type=pl.DeviceIdType.MESH,
            )
    lax.fori_loop(0, pairs, greet, 0)

    pack_tables(table_ref, tabs)
    edge = jnp.zeros((SUB, LANES), jnp.float32)
    blank = jnp.zeros((strips + 2 * SUB, LANES), jnp.float32)

    def widen(z, carry):
        for m in range(mats):
            wide[m] = mixed_ref[m, z].astype(jnp.float32)
            for y in range(lines):
                dens[m, z + 1, y + 1, 0:SUB, :] = edge
                dens[m, z + 1, y + 1, SUB + strips :, :] = edge
                for t in range(tiles):
                    line = wide[m, pl.ds(t * SUB * lines + y, SUB, stride=lines), :]
                    dens[m, z + 1, y + 1, SUB + t * SUB : 2 * SUB + t * SUB, :] = line
                    grid_ref[m, z, y, t] = line.astype(grid_ref.dtype)
        for side in range(2):
            @pl.when(jnp.logical_not(has_y[side]))
            def _():
                for m in range(mats):
                    dens[m, z + 1, side * (lines + 1)] = blank
        return carry

    lax.fori_loop(0, planes, widen, 0)
    for side in range(2):
        @pl.when(jnp.logical_not(has_z[side]))
        def _():
            for m in range(mats):
                for y in range(lines):
                    dens[m, side * (planes + 1), y + 1] = blank

    def level_step(j, carry):
        tile_levels(
            grid_ref, tabs, weight_ref, levels, j % lines, j // lines, 6.0 / depth_total / 255.0
        )
        return carry

    early = tiles * lines // 2
    lax.fori_loop(0, early, level_step, 0)

    others = pairs - 1
    for side in range(2):
        others = others + jnp.where(has_y[side], 1, 0) + jnp.where(has_z[side], 1, 0)
    pl.semaphore_wait(barrier, others)

    def z_copy(side):
        return pltpu.make_async_remote_copy(
            src_ref=grid_ref.at[:, (planes - 1) * side],
            dst_ref=z_in.at[1 - side],
            send_sem=z_send.at[side],
            recv_sem=z_recv.at[1 - side],
            device_id={"depth": z_peer[side]},
            device_id_type=pl.DeviceIdType.MESH,
        )

    def y_copy(side, t):
        return pltpu.make_async_remote_copy(
            src_ref=grid_ref.at[:, :, (lines - 1) * side, t],
            dst_ref=y_in.at[1 - side, t],
            send_sem=y_send.at[side, t],
            recv_sem=y_recv.at[1 - side, t],
            device_id={"tile": y_peer[side]},
            device_id_type=pl.DeviceIdType.MESH,
        )

    def rows_of_block(owner):
        return pl.ds(pl.multiple_of(owner * block, block), block)

    def pair_copy(chip):
        return pltpu.make_async_remote_copy(
            src_ref=image.at[rows_of_block(2 * chip + 1 - core)],
            dst_ref=pair_in.at[chip],
            send_sem=pair_send.at[chip],
            recv_sem=pair_recv.at[chip],
            device_id={"depth": partner},
            device_id_type=pl.DeviceIdType.MESH,
        )

    def block_copy(chip, source):
        return pltpu.make_async_remote_copy(
            src_ref=image.at[rows_of_block(2 * chip + core)],
            dst_ref=got.at[source],
            send_sem=send_sem.at[chip],
            recv_sem=recv_sem.at[source],
            device_id={"depth": 2 * chip + core},
            device_id_type=pl.DeviceIdType.MESH,
        )

    def forward(i):
        tile = far_first(mine, i, tiles)
        for k in range(half_tile):
            chip = tile * half_tile + k
            pair_copy(chip).wait_recv()
            start = (2 * chip + core) * block
            for s in range(block // stride):
                at = [
                    pl.ds(pl.multiple_of(start + (s * 4 + c) * group, group), group)
                    for c in range(4)
                ]
                ours = [image[at[c], :] for c in range(4)]
                theirs = [
                    pair_in[chip, (s * 4 + c) * group : (s * 4 + c + 1) * group, :]
                    for c in range(4)
                ]
                front = [jnp.where(core == 0, a, b) for a, b in zip(ours, theirs)]
                back = [jnp.where(core == 0, b, a) for a, b in zip(ours, theirs)]
                for c in range(3):
                    image[at[c], :] = front[c] + front[3] * back[c]
                image[at[3], :] = front[3] * back[3]

            @pl.when(chip != pair)
            def _():
                block_copy(chip, pair).start()

    for side in range(2):
        @pl.when(has_z[side])
        def _():
            z_copy(side).start()
    for i in range(tiles):
        for side in range(2):
            @pl.when(has_y[side])
            def _():
                y_copy(side, far_first(mine, i, tiles)).start()

    lax.fori_loop(early, tiles * lines, level_step, 0)

    for side in range(2):
        @pl.when(has_z[side])
        def _():
            z_copy(1 - side).wait_recv()
            for t in range(tiles):
                for m in range(mats):
                    for y in range(lines):
                        dens[
                            m, side * (planes + 1), y + 1, SUB + t * SUB : 2 * SUB + t * SUB, :
                        ] = z_in[side, m, y, t].astype(jnp.float32)

    def tile_step(i, carry):
        tile = far_first(mine, i, tiles)
        here = pl.ds(pl.multiple_of(tile * SUB + SUB, SUB), SUB)
        for side in range(2):
            @pl.when(has_y[side])
            def _():
                y_copy(1 - side, tile).wait_recv()
                for m in range(mats):
                    for z in range(planes):
                        dens[m, z + 1, side * (lines + 1), here, :] = y_in[
                            side, tile, m, z
                        ].astype(jnp.float32)

        def line_step(y, inner):
            sums, ahead = tile_image(
                dens, levels, weight_ref, y, tile, planes
            )
            for e in range(energies):
                for c in range(4):
                    value = sums[e][c] * (1.0 / 255.0) if c < 3 else ahead[e]
                    start = tile * (SUB * stride) + c * group + e * lines + y
                    image[pl.ds(start, SUB, stride=stride), :] = value
            return inner

        lax.fori_loop(0, lines, line_step, 0)
        for k in range(half_tile):
            pair_copy(tile * half_tile + k).start()

        @pl.when(i > 0)
        def _():
            forward(i - 1)
        return carry

    lax.fori_loop(0, tiles, tile_step, 0)
    forward(tiles - 1)
    got[pair] = image[rows_of_block(me), :]

    pieces = block // stride
    ahead = [None] * pieces
    sums = [[None] * 3 for _ in range(pieces)]
    for n in range(pairs):
        @pl.when(pair != n)
        def _():
            block_copy(n, n).wait_recv()
        for s in range(pieces):
            at = lambda c: got[n, (s * 4 + c) * group : (s * 4 + c + 1) * group, :]
            for c in range(3):
                sums[s][c] = at(c) if n == 0 else sums[s][c] + ahead[s] * at(c)
            ahead[s] = at(3) if n == 0 else ahead[s] * at(3)
    for s in range(pieces):
        for c in range(4):
            value = sums[s][c] if c < 3 else 1.0 - ahead[s]
            for e in range(energies):
                start = ((e * 4 + c) * pieces + s) * lines
                out_ref[start : start + lines, :] = value[e * lines : (e + 1) * lines, :]

    for side in range(2):
        @pl.when(has_z[side])
        def _():
            z_copy(side).wait_send()
        @pl.when(has_y[side])
        def _():
            for t in range(tiles):
                y_copy(side, t).wait_send()
    for n in range(pairs):
        pair_copy(n).wait_send()

        @pl.when(pair != n)
        def _():
            block_copy(n, n).wait_send()


def body(density, material_weight, color_table):
    mats, planes, lines, columns = density.shape
    energies = material_weight.shape[0]
    count = lax.axis_size("depth")
    strips = columns // LANES
    tiles = strips // SUB
    mixed = density.reshape(mats, planes, lines, strips, LANES).transpose(0, 1, 3, 2, 4)
    mixed = mixed.reshape(mats, planes, strips * lines, LANES)
    vmem = pl.BlockSpec(memory_space=pltpu.VMEM)
    total = strips * 4 * energies * lines
    own = columns // count
    dma = pltpu.SemaphoreType.DMA
    pixels = pl.pallas_call(
        functools.partial(render_kernel, planes * count),
        out_shape=pltpu.VMEM((total // count, LANES), jnp.float32),
        in_specs=[vmem, vmem, pl.BlockSpec(memory_space=pltpu.SMEM)],
        out_specs=vmem,
        scratch_shapes=[
            pltpu.VMEM((mats, planes, lines, tiles, SUB, LANES), density.dtype),
            pltpu.VMEM((mats, strips * lines, LANES), jnp.float32),
            pltpu.VMEM((mats, planes + 2, lines + 2, strips + 2 * SUB, LANES), jnp.float32),
            pltpu.VMEM((energies, 2, color_table.shape[2] // LANES, SUB, LANES), jnp.int32),
            pltpu.VMEM((lines, tiles, planes, energies * 4, SUB, LANES), jnp.float32),
            pltpu.VMEM((2, mats, lines, tiles, SUB, LANES), density.dtype),
            pltpu.VMEM((2, tiles, mats, planes, SUB, LANES), density.dtype),
            pltpu.VMEM((total, LANES), jnp.float32),
            pltpu.VMEM((count // 2, total // count, LANES), jnp.float32),
            pltpu.VMEM((count // 2, total // count, LANES), jnp.float32),
            dma((2,)), dma((2,)), dma((2, tiles)), dma((2, tiles)),
            dma((count // 2,)), dma((count // 2,)), dma((count // 2,)), dma((count // 2,)),
        ],
        compiler_params=pltpu.CompilerParams(collective_id=0, has_side_effects=True),
    )(mixed, color_table, material_weight)
    pixels = pixels.reshape(energies, 4, own // LANES, lines, LANES)
    return pixels.transpose(0, 1, 3, 2, 4).reshape(energies, 4, lines, own)


def solution(mesh):
    return jax.shard_map(
        body,
        mesh=mesh,
        in_specs=(P(None, "depth", "tile", None), P(), P()),
        out_specs=P(None, None, "tile", "depth"),
        check_vma=False,
    )
```

```python
import functools

import jax
import jax.numpy as jnp
from jax import lax
from jax.experimental import pallas as pl
from jax.experimental.pallas import tpu as pltpu
from jax.sharding import PartitionSpec as P

LANES = 128
SUB = 8


def pack_tables(table_ref, tabs):
    for e in range(table_ref.shape[0]):
        word = (
            table_ref[e, 0:1, :]
            + table_ref[e, 1:2, :] * 256
            + table_ref[e, 2:3, :] * 65536
            + lax.shift_left(table_ref[e, 3:4, :], 24)
        )
        bins = word.shape[1]
        pair = (word, pltpu.roll(word, bins - 1, 1))
        for k in range(2):
            for half in range(bins // LANES):
                tabs[e, k, half] = jnp.broadcast_to(
                    pair[k][:, half * LANES : (half + 1) * LANES], (SUB, LANES)
                )


def look_up(tabs, e, k, idx, where_half):
    found = None
    for half in range(tabs.shape[2]):
        piece = jnp.take_along_axis(tabs[e, k, half], idx, axis=1, mode="promise_in_bounds")
        found = piece if found is None else jnp.where(where_half == half, piece, found)
    return found


def channels_of(word):
    return (
        (word & 255).astype(jnp.float32),
        (lax.shift_right_logical(word, 8) & 255).astype(jnp.float32),
        (lax.shift_right_logical(word, 16) & 255).astype(jnp.float32),
        lax.shift_right_logical(word, 24).astype(jnp.float32),
    )


def mixer(weight_ref, e):
    w = [weight_ref[e, m] for m in range(weight_ref.shape[1])]

    def mix(values):
        total = w[0] * values[0]
        for m in range(1, len(values)):
            total = total + w[m] * values[m]
        return total

    return mix


def tile_levels(grid_ref, tabs, weight_ref, levels, y, tile, scale):
    mats, planes = grid_ref.shape[:2]
    for z in range(planes):
        mid = [grid_ref[m, z, y, tile].astype(jnp.float32) for m in range(mats)]
        for e in range(weight_ref.shape[0]):
            atten = mixer(weight_ref, e)(mid)
            level = 255.0 - 255.0 * jnp.exp(-0.5 * atten)
            bin_at = level.astype(jnp.int32)
            frac = level - bin_at.astype(jnp.float32)
            w1 = frac.astype(jnp.bfloat16).astype(jnp.float32)
            w0 = (1.0 - frac).astype(jnp.bfloat16).astype(jnp.float32)
            idx = bin_at & (LANES - 1)
            half = lax.shift_right_logical(bin_at, 7)
            low = channels_of(look_up(tabs, e, 0, idx, half))
            high = channels_of(look_up(tabs, e, 1, idx, half))
            for c in range(4):
                value = w0 * low[c] + w1 * high[c]
                levels[y, tile, z, e * 4 + c] = value * scale if c == 3 else value


def tile_image(dens, levels, weight_ref, y, tile, planes):
    mats = dens.shape[0]
    energies = weight_ref.shape[0]
    lane = lax.broadcasted_iota(jnp.int32, (SUB, LANES), 1)
    first, last = lane == 0, lane == LANES - 1
    base = tile * SUB + SUB
    rows = pl.ds(pl.multiple_of(base, SUB), SUB)
    ahead = [None] * energies
    sums = [[None] * 3 for _ in range(energies)]
    for z in range(planes):
        dz, dy, dx = [], [], []
        for m in range(mats):
            here = dens[m, z + 1, y + 1, rows, :]
            dz.append(dens[m, z + 2, y + 1, rows, :] - dens[m, z, y + 1, rows, :])
            dy.append(dens[m, z + 1, y + 2, rows, :] - dens[m, z + 1, y, rows, :])
            above = dens[m, z + 1, y + 1, pl.ds(base - 1, SUB), :]
            below = dens[m, z + 1, y + 1, pl.ds(base + 1, SUB), :]
            right = pltpu.roll(jnp.where(first, below, here), LANES - 1, 1)
            left = pltpu.roll(jnp.where(last, above, here), 1, 1)
            dx.append(right - left)
        for e in range(energies):
            mix = mixer(weight_ref, e)
            gz, gy, gx = mix(dz) * 0.5, mix(dy) * 0.5, mix(dx) * 0.5
            sq = gz * gz + gy * gy + gx * gx
            inv = lax.rsqrt(sq + 1.0)
            shading = 0.3 + 0.7 * jnp.abs(0.8 * gz + 0.48 * gy + 0.36 * gx) * inv
            opacity = levels[y, tile, z, e * 4 + 3] * (sq * inv * inv)
            lit = opacity * shading
            if z:
                lit = lit * ahead[e]
            for c in range(3):
                term = lit * levels[y, tile, z, e * 4 + c]
                sums[e][c] = term if z == 0 else sums[e][c] + term
            transmit = 1.0 - opacity
            ahead[e] = transmit if z == 0 else ahead[e] * transmit
    return sums, ahead


def far_first(mine, step, tiles):
    if tiles & (tiles - 1):
        return (mine + 1 + step) % tiles
    other, result, bit = tiles - 1 - step, 0, 1
    while bit < tiles:
        result = result + bit * ((mine // bit + other // bit) % 2)
        bit *= 2
    return result


WIRE_STEPS = 64000.0
WIRE_ZERO = 32768


def to_wire(value):
    root = jnp.sqrt(jnp.sqrt(jnp.maximum(value, 0.0)))
    return (root * WIRE_STEPS + 0.5).astype(jnp.int32) - WIRE_ZERO


def from_wire(code):
    root = (code.astype(jnp.float32) + float(WIRE_ZERO)) * (1.0 / WIRE_STEPS)
    root = root * root
    return root * root


def render_kernel(
    depth_total, mixed_hbm, table_hbm, weight_hbm, out_ref,
    mixed_ref, table_ref, weight_ref,
    grid_ref, wide, dens, tabs, levels, z_in, y_in, image, pair_in, packed, got,
    in_sem, up_sem, down_sem, side_sem,
    z_send, z_recv, y_send, y_recv, pair_send, pair_recv, send_sem, recv_sem,
):
    mats, planes, lines, tiles = grid_ref.shape[:4]
    strips = tiles * SUB
    energies = weight_ref.shape[0]
    _, pairs, block, _ = got.shape
    count = 2 * pairs
    per_tile = count // tiles
    half_tile = per_tile // 2
    stride = 4 * energies
    pieces = block // stride
    line_rows = strips * stride
    me, row = lax.axis_index("depth"), lax.axis_index("tile")
    rows_of = lax.axis_size("tile")
    has_z = (me > 0, me < count - 1)
    has_y = (row > 0, row < rows_of - 1)
    z_peer = (me - 1, me + 1)
    y_peer = (row - 1, row + 1)
    mine = me // per_tile
    core, pair = me % 2, me // 2
    partner = me + 1 - 2 * core
    beside = me + 2 - 4 * (pair % 2)
    layers = pairs // 2
    layer = pair // 2
    has_layer = (layer > 0, layer < layers - 1)
    layer_peer = (me - 4, me + 4)
    first_line = jnp.where(has_y[0], 1, 0)

    def line_of(k):
        return (k + first_line) % lines

    loads = (
        pltpu.make_async_copy(mixed_hbm, mixed_ref, in_sem.at[0]),
        pltpu.make_async_copy(table_hbm, table_ref, in_sem.at[1]),
        pltpu.make_async_copy(weight_hbm, weight_ref, in_sem.at[2]),
    )
    for load in loads:
        load.start()

    barrier = pltpu.get_barrier_semaphore()

    def tell(semaphore, **device):
        pl.semaphore_signal(
            semaphore, inc=1, device_id=device, device_id_type=pl.DeviceIdType.MESH
        )

    tell(barrier, depth=partner)
    tell(barrier, depth=beside)
    others = 2
    outer = me - 1 + 2 * core
    has_outer = jnp.logical_and(outer >= 0, outer < count)

    @pl.when(has_outer)
    def _():
        tell(barrier, depth=outer)
    others = others + jnp.where(has_outer, 1, 0)
    for side in range(2):
        @pl.when(has_y[side])
        def _():
            tell(barrier, tile=y_peer[side])

        @pl.when(has_layer[side])
        def _():
            tell(barrier, depth=layer_peer[side])
        others = others + jnp.where(has_y[side], 1, 0) + jnp.where(has_layer[side], 1, 0)

    edge = jnp.zeros((SUB, LANES), jnp.float32)
    blank = jnp.zeros((strips + 2 * SUB, LANES), jnp.float32)
    for side in range(2):
        @pl.when(jnp.logical_not(has_z[side]))
        def _():
            for m in range(mats):
                for y in range(lines):
                    dens[m, side * (planes + 1), y + 1] = blank
    loads[0].wait()

    def widen(z, carry):
        for m in range(mats):
            wide[m] = mixed_ref[m, z].astype(jnp.float32)
            for y in range(lines):
                dens[m, z + 1, y + 1, 0:SUB, :] = edge
                dens[m, z + 1, y + 1, SUB + strips :, :] = edge
                for t in range(tiles):
                    line = wide[m, pl.ds(t * SUB * lines + y, SUB, stride=lines), :]
                    dens[m, z + 1, y + 1, SUB + t * SUB : 2 * SUB + t * SUB, :] = line
                    grid_ref[m, z, y, t] = line.astype(grid_ref.dtype)
        for side in range(2):
            @pl.when(jnp.logical_not(has_y[side]))
            def _():
                for m in range(mats):
                    dens[m, z + 1, side * (lines + 1)] = blank
        return carry

    lax.fori_loop(0, planes, widen, 0)
    pl.semaphore_wait(barrier, others)

    def z_copy(side):
        return pltpu.make_async_remote_copy(
            src_ref=grid_ref.at[:, (planes - 1) * side],
            dst_ref=z_in.at[1 - side],
            send_sem=z_send.at[side],
            recv_sem=z_recv.at[1 - side],
            device_id={"depth": z_peer[side]},
            device_id_type=pl.DeviceIdType.MESH,
        )

    def y_copy(side, t):
        return pltpu.make_async_remote_copy(
            src_ref=grid_ref.at[:, :, (lines - 1) * side, t],
            dst_ref=y_in.at[1 - side, t],
            send_sem=y_send.at[side, t],
            recv_sem=y_recv.at[1 - side, t],
            device_id={"tile": y_peer[side]},
            device_id_type=pl.DeviceIdType.MESH,
        )

    def rows_of_block(y, owner):
        return pl.ds(pl.multiple_of(y * line_rows + owner * block, block), block)

    def pair_copy(y, chip):
        return pltpu.make_async_remote_copy(
            src_ref=image.at[rows_of_block(y, 2 * chip + 1 - core)],
            dst_ref=pair_in.at[y, chip],
            send_sem=pair_send.at[y, chip],
            recv_sem=pair_recv.at[y, chip],
            device_id={"depth": partner},
            device_id_type=pl.DeviceIdType.MESH,
        )

    def block_copy(y, chip, source):
        return pltpu.make_async_remote_copy(
            src_ref=packed.at[y, chip],
            dst_ref=got.at[y, source],
            send_sem=send_sem.at[y, chip],
            recv_sem=recv_sem.at[y, source],
            device_id={"depth": 2 * chip + core},
            device_id_type=pl.DeviceIdType.MESH,
        )

    upper = lax.broadcasted_iota(jnp.int32, (SUB, LANES), 0) < energies

    def both_halves(value):
        return jnp.where(upper, pltpu.roll(value, energies, 0), value)

    def forward(k):
        y, tile = line_of(k // tiles), far_first(mine, k % tiles, tiles)
        for h in range(half_tile):
            chip = tile * half_tile + h
            pair_copy(y, chip).wait_recv()
            start = y * line_rows + (2 * chip + core) * block
            for s in range(pieces):
                front, back = [], []
                for v in range(2):
                    at = s * stride + v * SUB
                    ours = image[pl.ds(pl.multiple_of(start + at, SUB), SUB), :]
                    theirs = pair_in[y, chip, at : at + SUB, :]
                    front.append(jnp.where(core == 0, ours, theirs))
                    back.append(jnp.where(core == 0, theirs, ours))
                clear = both_halves(front[1])
                low = front[0] + clear * back[0]
                high = jnp.where(upper, front[1], 0.0) + clear * back[1]
                high = jnp.where(upper, high, 1.0 - high)
                packed[y, chip, s * stride : (s + 1) * stride, :] = to_wire(
                    jnp.concatenate([low, high], axis=0)
                ).astype(packed.dtype)

            @pl.when(chip != pair)
            def _():
                block_copy(y, chip, pair).start()

    for i in range(tiles):
        for side in range(2):
            @pl.when(has_y[side])
            def _():
                y_copy(side, far_first(mine, i, tiles)).start()
        if i == 0:
            for side in range(2):
                @pl.when(has_z[side])
                def _():
                    z_copy(side).start()

    loads[1].wait()
    loads[2].wait()
    pack_tables(table_ref, tabs)
    steps = tiles * lines
    every = max(1, steps // layers)

    def pass_on(p):
        for side, (turn, semaphore) in enumerate(((layers - 1 - layer, down_sem), (layer, up_sem))):
            @pl.when(jnp.logical_and(turn == p, has_layer[1 - side]))
            def _():
                pl.semaphore_wait(semaphore, 1)

            @pl.when(jnp.logical_and(turn == p, has_layer[side]))
            def _():
                tell(semaphore, depth=layer_peer[side])

    def level_step(j, carry):
        for p in range(layers):
            if p * every < steps:
                @pl.when(j == p * every)
                def _():
                    pass_on(p)
        tile_levels(
            grid_ref, tabs, weight_ref, levels, line_of(j // tiles), j % tiles,
            6.0 / depth_total / 255.0,
        )
        return carry

    lax.fori_loop(0, steps, level_step, 0)
    for p in range(layers):
        if p * every >= steps:
            pass_on(p)
    tell(side_sem, depth=beside)

    for side in range(2):
        @pl.when(has_z[side])
        def _():
            z_copy(1 - side).wait_recv()
            for t in range(tiles):
                for m in range(mats):
                    for y in range(lines):
                        dens[
                            m, side * (planes + 1), y + 1, SUB + t * SUB : 2 * SUB + t * SUB, :
                        ] = z_in[side, m, y, t].astype(jnp.float32)

    def image_step(k, carry):
        y, tile = line_of(k // tiles), far_first(mine, k % tiles, tiles)
        here = pl.ds(pl.multiple_of(tile * SUB + SUB, SUB), SUB)
        for side in range(2):
            @pl.when(jnp.logical_and(has_y[side], y == side * (lines - 1)))
            def _():
                y_copy(1 - side, tile).wait_recv()
                for m in range(mats):
                    for z in range(planes):
                        dens[m, z + 1, side * (lines + 1), here, :] = y_in[
                            side, tile, m, z
                        ].astype(jnp.float32)

        sums, ahead = tile_image(dens, levels, weight_ref, y, tile, planes)
        for e in range(energies):
            for c in range(4):
                value = sums[e][c] * (1.0 / 255.0) if c < 3 else ahead[e]
                start = y * line_rows + tile * (SUB * stride) + c * energies + e
                image[pl.ds(start, SUB, stride=stride), :] = value
        for h in range(half_tile):
            pair_copy(y, tile * half_tile + h).start()

        @pl.when(k == 1)
        def _():
            pl.semaphore_wait(side_sem, 1)

        @pl.when(k > 0)
        def _():
            forward(k - 1)
        return carry

    lax.fori_loop(0, steps, image_step, 0)
    forward(steps - 1)
    for y in range(lines):
        got[y, pair] = packed[y, pair]

    for k in range(lines):
        y = line_of(k)
        low, high, clear = [None] * pieces, [None] * pieces, [None] * pieces
        for n in range(pairs):
            @pl.when(pair != n)
            def _():
                block_copy(y, n, n).wait_recv()
            for s in range(pieces):
                both = from_wire(
                    got[y, n, s * stride : (s + 1) * stride, :].astype(jnp.int32)
                )
                a, b = both[0:SUB], both[SUB:]
                seen = both_halves(1.0 - b)
                low[s] = a if n == 0 else low[s] + clear[s] * a
                high[s] = b if n == 0 else high[s] + clear[s] * b
                clear[s] = seen if n == 0 else clear[s] * seen
        for s in range(pieces):
            parts = (low[s], jnp.where(upper, high[s], 1.0 - clear[s]))
            for c in range(4):
                value = parts[c // 2][(c % 2) * energies : (c % 2 + 1) * energies]
                out_ref[
                    pl.ds((c * pieces + s) * lines + y, energies, stride=4 * pieces * lines), :
                ] = value

    for side in range(2):
        @pl.when(has_z[side])
        def _():
            z_copy(side).wait_send()
        @pl.when(has_y[side])
        def _():
            for t in range(tiles):
                y_copy(side, t).wait_send()
    for y in range(lines):
        for n in range(pairs):
            pair_copy(y, n).wait_send()

            @pl.when(pair != n)
            def _():
                block_copy(y, n, n).wait_send()


def body(density, material_weight, color_table):
    mats, planes, lines, columns = density.shape
    energies = material_weight.shape[0]
    count = lax.axis_size("depth")
    strips = columns // LANES
    tiles = strips // SUB
    mixed = density.reshape(mats, planes, lines, strips, LANES).transpose(0, 1, 3, 2, 4)
    mixed = mixed.reshape(mats, planes, strips * lines, LANES)
    hbm = pl.BlockSpec(memory_space=pl.ANY)
    total = strips * 4 * energies * lines
    own = columns // count
    block = total // count // lines
    pairs = count // 2
    dma = pltpu.SemaphoreType.DMA
    flag = pltpu.SemaphoreType.REGULAR
    wire = jnp.int16
    pixels = pl.pallas_call(
        functools.partial(render_kernel, planes * count),
        out_shape=pltpu.VMEM((total // count, LANES), jnp.float32),
        in_specs=[hbm, hbm, hbm],
        out_specs=pl.BlockSpec(memory_space=pltpu.VMEM),
        scratch_shapes=[
            pltpu.VMEM(mixed.shape, density.dtype),
            pltpu.VMEM(color_table.shape, color_table.dtype),
            pltpu.SMEM(material_weight.shape, material_weight.dtype),
            pltpu.VMEM((mats, planes, lines, tiles, SUB, LANES), density.dtype),
            pltpu.VMEM((mats, strips * lines, LANES), jnp.float32),
            pltpu.VMEM((mats, planes + 2, lines + 2, strips + 2 * SUB, LANES), jnp.float32),
            pltpu.VMEM((energies, 2, color_table.shape[2] // LANES, SUB, LANES), jnp.int32),
            pltpu.VMEM((lines, tiles, planes, energies * 4, SUB, LANES), jnp.float32),
            pltpu.VMEM((2, mats, lines, tiles, SUB, LANES), density.dtype),
            pltpu.VMEM((2, tiles, mats, planes, SUB, LANES), density.dtype),
            pltpu.VMEM((total, LANES), jnp.float32),
            pltpu.VMEM((lines, pairs, block, LANES), jnp.float32),
            pltpu.VMEM((lines, pairs, block, LANES), wire),
            pltpu.VMEM((lines, pairs, block, LANES), wire),
            dma((3,)), flag, flag, flag,
            dma((2,)), dma((2,)), dma((2, tiles)), dma((2, tiles)),
            dma((lines, pairs)), dma((lines, pairs)), dma((lines, pairs)), dma((lines, pairs)),
        ],
        compiler_params=pltpu.CompilerParams(collective_id=0, has_side_effects=True),
    )(mixed, color_table, material_weight)
    pixels = pixels.reshape(energies, 4, own // LANES, lines, LANES)
    return pixels.transpose(0, 1, 3, 2, 4).reshape(energies, 4, lines, own)


def solution(mesh):
    return jax.shard_map(
        body,
        mesh=mesh,
        in_specs=(P(None, "depth", "tile", None), P(), P()),
        out_specs=P(None, None, "tile", "depth"),
        check_vma=False,
    )
```

```python
import functools

import jax
import jax.numpy as jnp
from jax import lax
from jax.experimental import pallas as pl
from jax.experimental.pallas import tpu as pltpu
from jax.sharding import PartitionSpec as P

LANES = 128
SUB = 8
LAG = 4
LOG2_E = 1.4426950408889634
PICK = lax.GatherDimensionNumbers(
    offset_dims=(),
    collapsed_slice_dims=(1,),
    start_index_map=(1,),
    operand_batching_dims=(0,),
    start_indices_batching_dims=(0,),
)


def pack_tables(table_ref, tabs):
    for e in range(table_ref.shape[0]):
        word = (
            table_ref[e, 0:1, :]
            + table_ref[e, 1:2, :] * 256
            + table_ref[e, 2:3, :] * 65536
            + lax.shift_left(table_ref[e, 3:4, :], 24)
        )
        bins = word.shape[1]
        pair = (word, pltpu.roll(word, bins - 1, 1))
        for k in range(2):
            for half in range(bins // LANES):
                tabs[e, k, half] = jnp.broadcast_to(
                    pair[k][:, half * LANES : (half + 1) * LANES], (SUB, LANES)
                )


def look_up(tabs, e, k, idx, where_half):
    found = None
    for half in range(tabs.shape[2]):
        piece = lax.gather(
            tabs[e, k, half], idx[:, :, None], PICK, (1, 1),
            mode=lax.GatherScatterMode.PROMISE_IN_BOUNDS,
        )
        found = piece if found is None else jnp.where(where_half == half, piece, found)
    return found


def channels_of(word):
    return (
        (word & 255).astype(jnp.float32),
        (lax.shift_right_logical(word, 8) & 255).astype(jnp.float32),
        (lax.shift_right_logical(word, 16) & 255).astype(jnp.float32),
        lax.shift_right_logical(word, 24).astype(jnp.float32),
    )


def mixer(weight_ref, e):
    w = [weight_ref[e, m] for m in range(weight_ref.shape[1])]

    def mix(values):
        total = w[0] * values[0]
        for m in range(1, len(values)):
            total = total + w[m] * values[m]
        return total

    return mix


def tile_levels(grid_ref, tabs, weight_ref, atten_ref, levels, y, tile, scale):
    mats, planes = grid_ref.shape[:2]
    rows = pl.ds(pl.multiple_of(tile * SUB + SUB, SUB), SUB)
    for z in range(planes):
        mid = [grid_ref[m, z, y, tile].astype(jnp.float32) for m in range(mats)]
        for e in range(weight_ref.shape[0]):
            atten = mixer(weight_ref, e)(mid)
            atten_ref[e, z + 1, y + 1, rows, :] = atten
            level = 255.0 - 255.0 * jnp.exp2((-0.5 * LOG2_E) * atten)
            bin_at = level.astype(jnp.int32)
            frac = level - bin_at.astype(jnp.float32)
            w1 = frac.astype(jnp.bfloat16).astype(jnp.float32)
            w0 = (1.0 - frac).astype(jnp.bfloat16).astype(jnp.float32)
            idx = bin_at & (LANES - 1)
            half = lax.shift_right_logical(bin_at, 7)
            low = channels_of(look_up(tabs, e, 0, idx, half))
            high = channels_of(look_up(tabs, e, 1, idx, half))
            for c in range(4):
                value = w0 * low[c] + w1 * high[c]
                levels[y, tile, z, e * 4 + c] = value * scale if c == 3 else value


def tile_image(atten_ref, levels, y, tile, planes):
    energies = atten_ref.shape[0]
    lane = lax.broadcasted_iota(jnp.int32, (SUB, LANES), 1)
    first, last = lane == 0, lane == LANES - 1
    base = tile * SUB + SUB
    rows = pl.ds(pl.multiple_of(base, SUB), SUB)
    sums, ahead = [], []
    for e in range(energies):
        clear, total = None, [None] * 3
        for z in range(planes):
            here = atten_ref[e, z + 1, y + 1, rows, :]
            dz = atten_ref[e, z + 2, y + 1, rows, :] - atten_ref[e, z, y + 1, rows, :]
            dy = atten_ref[e, z + 1, y + 2, rows, :] - atten_ref[e, z + 1, y, rows, :]
            above = atten_ref[e, z + 1, y + 1, pl.ds(base - 1, SUB), :]
            below = atten_ref[e, z + 1, y + 1, pl.ds(base + 1, SUB), :]
            right = pltpu.roll(jnp.where(first, below, here), LANES - 1, 1)
            left = pltpu.roll(jnp.where(last, above, here), 1, 1)
            dx = right - left
            sq = dz * dz + dy * dy + dx * dx
            inv = lax.rsqrt(sq + 4.0)
            shading = 0.3 + jnp.abs(0.56 * dz + 0.336 * dy + 0.252 * dx) * inv
            opacity = levels[y, tile, z, e * 4 + 3] * (sq * inv * inv)
            lit = opacity * shading
            if z:
                lit = lit * clear
            for c in range(3):
                term = lit * levels[y, tile, z, e * 4 + c]
                total[c] = term if z == 0 else total[c] + term
            transmit = 1.0 - opacity
            clear = transmit if z == 0 else clear * transmit
        sums.append(total)
        ahead.append(clear)
    return sums, ahead


def far_first(mine, step, tiles):
    if tiles & (tiles - 1):
        return (mine + 1 + step) % tiles
    other, result, bit = tiles - 1 - step, 0, 1
    while bit < tiles:
        result = result + bit * ((mine // bit + other // bit) % 2)
        bit *= 2
    return result


WIRE_STEPS = 64000.0
WIRE_ZERO = 32768


def to_wire(value):
    root = jnp.sqrt(jnp.sqrt(jnp.maximum(value, 0.0)))
    return (root * WIRE_STEPS + 0.5).astype(jnp.int32) - WIRE_ZERO


def from_wire(code):
    root = (code.astype(jnp.float32) + float(WIRE_ZERO)) * (1.0 / WIRE_STEPS)
    root = root * root
    return root * root


def render_kernel(
    depth_total, mixed_hbm, table_hbm, weight_hbm, out_ref,
    mixed_ref, table_ref, weight_ref,
    grid_ref, wide, atten_ref, tabs, levels, z_in, y_in, image, pair_in, packed, got,
    in_sem, up_sem, down_sem, side_sem,
    z_send, z_recv, y_send, y_recv, pair_send, pair_recv, send_sem, recv_sem,
):
    mats, planes, lines, tiles = grid_ref.shape[:4]
    strips = tiles * SUB
    energies = weight_ref.shape[0]
    _, pairs, block, _ = got.shape
    count = 2 * pairs
    per_tile = count // tiles
    half_tile = per_tile // 2
    stride = 4 * energies
    pieces = block // stride
    line_rows = strips * stride
    me, row = lax.axis_index("depth"), lax.axis_index("tile")
    rows_of = lax.axis_size("tile")
    has_z = (me > 0, me < count - 1)
    has_y = (row > 0, row < rows_of - 1)
    z_peer = (me - 1, me + 1)
    y_peer = (row - 1, row + 1)
    mine = me // per_tile
    core, pair = me % 2, me // 2
    partner = me + 1 - 2 * core
    beside = me + 2 - 4 * (pair % 2)
    layers = pairs // 2
    layer = pair // 2
    has_layer = (layer > 0, layer < layers - 1)
    layer_peer = (me - 4, me + 4)
    first_line = jnp.where(has_y[0], 1, 0)

    def line_of(k):
        return (k + first_line) % lines

    loads = (
        pltpu.make_async_copy(mixed_hbm, mixed_ref, in_sem.at[0]),
        pltpu.make_async_copy(table_hbm, table_ref, in_sem.at[1]),
        pltpu.make_async_copy(weight_hbm, weight_ref, in_sem.at[2]),
    )
    for load in loads:
        load.start()

    barrier = pltpu.get_barrier_semaphore()

    def tell(semaphore, **device):
        pl.semaphore_signal(
            semaphore, inc=1, device_id=device, device_id_type=pl.DeviceIdType.MESH
        )

    tell(barrier, depth=partner)
    tell(barrier, depth=beside)
    others = 2
    outer = me - 1 + 2 * core
    has_outer = jnp.logical_and(outer >= 0, outer < count)

    @pl.when(has_outer)
    def _():
        tell(barrier, depth=outer)
    others = others + jnp.where(has_outer, 1, 0)
    for side in range(2):
        @pl.when(has_y[side])
        def _():
            tell(barrier, tile=y_peer[side])

        @pl.when(has_layer[side])
        def _():
            tell(barrier, depth=layer_peer[side])
        others = others + jnp.where(has_y[side], 1, 0) + jnp.where(has_layer[side], 1, 0)

    edge = jnp.zeros((SUB, LANES), jnp.float32)
    blank = jnp.zeros((strips + 2 * SUB, LANES), jnp.float32)

    def clear_edges(z, carry):
        for e in range(energies):
            for y in range(lines):
                atten_ref[e, z + 1, y + 1, 0:SUB, :] = edge
                atten_ref[e, z + 1, y + 1, SUB + strips :, :] = edge
        for side in range(2):
            @pl.when(jnp.logical_not(has_y[side]))
            def _():
                for e in range(energies):
                    atten_ref[e, z + 1, side * (lines + 1)] = blank
        return carry

    lax.fori_loop(0, planes, clear_edges, 0)
    for side in range(2):
        @pl.when(jnp.logical_not(has_z[side]))
        def _():
            for e in range(energies):
                for y in range(lines):
                    atten_ref[e, side * (planes + 1), y + 1] = blank
    loads[0].wait()

    def widen(z, carry):
        for m in range(mats):
            wide[m] = mixed_ref[m, z].astype(jnp.float32)
            for y in range(lines):
                for t in range(tiles):
                    line = wide[m, pl.ds(t * SUB * lines + y, SUB, stride=lines), :]
                    grid_ref[m, z, y, t] = line.astype(grid_ref.dtype)
        return carry

    lax.fori_loop(0, planes, widen, 0)
    pl.semaphore_wait(barrier, others)

    def z_copy(side):
        return pltpu.make_async_remote_copy(
            src_ref=grid_ref.at[:, (planes - 1) * side],
            dst_ref=z_in.at[1 - side],
            send_sem=z_send.at[side],
            recv_sem=z_recv.at[1 - side],
            device_id={"depth": z_peer[side]},
            device_id_type=pl.DeviceIdType.MESH,
        )

    def y_copy(side, t):
        return pltpu.make_async_remote_copy(
            src_ref=grid_ref.at[:, :, (lines - 1) * side, t],
            dst_ref=y_in.at[1 - side, t],
            send_sem=y_send.at[side, t],
            recv_sem=y_recv.at[1 - side, t],
            device_id={"tile": y_peer[side]},
            device_id_type=pl.DeviceIdType.MESH,
        )

    def rows_of_block(y, owner):
        return pl.ds(pl.multiple_of(y * line_rows + owner * block, block), block)

    def pair_copy(y, chip):
        return pltpu.make_async_remote_copy(
            src_ref=image.at[rows_of_block(y, 2 * chip + 1 - core)],
            dst_ref=pair_in.at[y, chip],
            send_sem=pair_send.at[y, chip],
            recv_sem=pair_recv.at[y, chip],
            device_id={"depth": partner},
            device_id_type=pl.DeviceIdType.MESH,
        )

    def block_copy(y, chip, source):
        return pltpu.make_async_remote_copy(
            src_ref=packed.at[y, chip],
            dst_ref=got.at[y, source],
            send_sem=send_sem.at[y, chip],
            recv_sem=recv_sem.at[y, source],
            device_id={"depth": 2 * chip + core},
            device_id_type=pl.DeviceIdType.MESH,
        )

    upper = lax.broadcasted_iota(jnp.int32, (SUB, LANES), 0) < energies

    def both_halves(value):
        return jnp.where(upper, pltpu.roll(value, energies, 0), value)

    def forward(k):
        y, tile = line_of(k // tiles), far_first(mine, k % tiles, tiles)
        for h in range(half_tile):
            chip = tile * half_tile + h
            pair_copy(y, chip).wait_recv()
            start = y * line_rows + (2 * chip + core) * block
            for s in range(pieces):
                front, back = [], []
                for v in range(2):
                    at = s * stride + v * SUB
                    ours = image[pl.ds(pl.multiple_of(start + at, SUB), SUB), :]
                    theirs = pair_in[y, chip, at : at + SUB, :]
                    front.append(jnp.where(core == 0, ours, theirs))
                    back.append(jnp.where(core == 0, theirs, ours))
                clear = both_halves(front[1])
                low = front[0] + clear * back[0]
                high = jnp.where(upper, front[1], 0.0) + clear * back[1]
                high = jnp.where(upper, high, 1.0 - high)
                packed[y, chip, s * stride : (s + 1) * stride, :] = to_wire(
                    jnp.concatenate([low, high], axis=0)
                ).astype(packed.dtype)

            @pl.when(chip != pair)
            def _():
                block_copy(y, chip, pair).start()

    for i in range(tiles):
        for side in range(2):
            @pl.when(has_y[side])
            def _():
                y_copy(side, far_first(mine, i, tiles)).start()
        if i == 0:
            for side in range(2):
                @pl.when(has_z[side])
                def _():
                    z_copy(side).start()

    loads[1].wait()
    loads[2].wait()
    pack_tables(table_ref, tabs)
    steps = tiles * lines
    every = max(1, steps // layers)
    lag = min(LAG, steps - 1)

    def pass_on(p):
        for side, (turn, semaphore) in enumerate(((layers - 1 - layer, down_sem), (layer, up_sem))):
            @pl.when(jnp.logical_and(turn == p, has_layer[1 - side]))
            def _():
                pl.semaphore_wait(semaphore, 1)

            @pl.when(jnp.logical_and(turn == p, has_layer[side]))
            def _():
                tell(semaphore, depth=layer_peer[side])

    def level_step(j, carry):
        for p in range(layers):
            if p * every < steps:
                @pl.when(j == p * every)
                def _():
                    pass_on(p)
        tile_levels(
            grid_ref, tabs, weight_ref, atten_ref, levels, line_of(j // tiles), j % tiles,
            6.0 / depth_total / 255.0,
        )
        return carry

    lax.fori_loop(0, steps, level_step, 0)
    for p in range(layers):
        if p * every >= steps:
            pass_on(p)
    tell(side_sem, depth=beside)

    for side in range(2):
        @pl.when(has_z[side])
        def _():
            z_copy(1 - side).wait_recv()
            for t in range(tiles):
                for y in range(lines):
                    mid = [z_in[side, m, y, t].astype(jnp.float32) for m in range(mats)]
                    for e in range(energies):
                        atten_ref[
                            e, side * (planes + 1), y + 1, SUB + t * SUB : 2 * SUB + t * SUB, :
                        ] = mixer(weight_ref, e)(mid)

    def image_step(k, carry):
        @pl.when(k == lag)
        def _():
            pl.semaphore_wait(side_sem, 1)

        @pl.when(k >= lag)
        def _():
            forward(k - lag)

        y, tile = line_of(k // tiles), far_first(mine, k % tiles, tiles)
        here = pl.ds(pl.multiple_of(tile * SUB + SUB, SUB), SUB)
        for side in range(2):
            @pl.when(jnp.logical_and(has_y[side], y == side * (lines - 1)))
            def _():
                y_copy(1 - side, tile).wait_recv()
                for z in range(planes):
                    mid = [y_in[side, tile, m, z].astype(jnp.float32) for m in range(mats)]
                    for e in range(energies):
                        atten_ref[e, z + 1, side * (lines + 1), here, :] = mixer(weight_ref, e)(mid)

        sums, ahead = tile_image(atten_ref, levels, y, tile, planes)
        for e in range(energies):
            for c in range(4):
                value = sums[e][c] * (1.0 / 255.0) if c < 3 else ahead[e]
                start = y * line_rows + tile * (SUB * stride) + c * energies + e
                image[pl.ds(start, SUB, stride=stride), :] = value
        for h in range(half_tile):
            pair_copy(y, tile * half_tile + h).start()

        return carry

    lax.fori_loop(0, steps, image_step, 0)

    def late_step(k, carry):
        forward(k)
        return carry

    lax.fori_loop(steps - lag, steps, late_step, 0)
    for y in range(lines):
        got[y, pair] = packed[y, pair]

    for k in range(lines):
        y = line_of(k)
        low, high, clear = [None] * pieces, [None] * pieces, [None] * pieces
        for n in range(pairs):
            @pl.when(pair != n)
            def _():
                block_copy(y, n, n).wait_recv()
            for s in range(pieces):
                both = from_wire(
                    got[y, n, s * stride : (s + 1) * stride, :].astype(jnp.int32)
                )
                a, b = both[0:SUB], both[SUB:]
                seen = both_halves(1.0 - b)
                low[s] = a if n == 0 else low[s] + clear[s] * a
                high[s] = b if n == 0 else high[s] + clear[s] * b
                clear[s] = seen if n == 0 else clear[s] * seen
        for s in range(pieces):
            parts = (low[s], jnp.where(upper, high[s], 1.0 - clear[s]))
            for c in range(4):
                value = parts[c // 2][(c % 2) * energies : (c % 2 + 1) * energies]
                out_ref[
                    pl.ds((c * pieces + s) * lines + y, energies, stride=4 * pieces * lines), :
                ] = value

    for side in range(2):
        @pl.when(has_z[side])
        def _():
            z_copy(side).wait_send()
        @pl.when(has_y[side])
        def _():
            for t in range(tiles):
                y_copy(side, t).wait_send()
    for y in range(lines):
        for n in range(pairs):
            pair_copy(y, n).wait_send()

            @pl.when(pair != n)
            def _():
                block_copy(y, n, n).wait_send()


def body(density, material_weight, color_table):
    mats, planes, lines, columns = density.shape
    energies = material_weight.shape[0]
    count = lax.axis_size("depth")
    strips = columns // LANES
    tiles = strips // SUB
    mixed = density.reshape(mats, planes, lines, strips, LANES).transpose(0, 1, 3, 2, 4)
    mixed = mixed.reshape(mats, planes, strips * lines, LANES)
    hbm = pl.BlockSpec(memory_space=pl.ANY)
    total = strips * 4 * energies * lines
    own = columns // count
    block = total // count // lines
    pairs = count // 2
    dma = pltpu.SemaphoreType.DMA
    flag = pltpu.SemaphoreType.REGULAR
    wire = jnp.int16
    pixels = pl.pallas_call(
        functools.partial(render_kernel, planes * count),
        out_shape=pltpu.VMEM((total // count, LANES), jnp.float32),
        in_specs=[hbm, hbm, hbm],
        out_specs=pl.BlockSpec(memory_space=pltpu.VMEM),
        scratch_shapes=[
            pltpu.VMEM(mixed.shape, density.dtype),
            pltpu.VMEM(color_table.shape, color_table.dtype),
            pltpu.SMEM(material_weight.shape, material_weight.dtype),
            pltpu.VMEM((mats, planes, lines, tiles, SUB, LANES), density.dtype),
            pltpu.VMEM((mats, strips * lines, LANES), jnp.float32),
            pltpu.VMEM((energies, planes + 2, lines + 2, strips + 2 * SUB, LANES), jnp.float32),
            pltpu.VMEM((energies, 2, color_table.shape[2] // LANES, SUB, LANES), jnp.int32),
            pltpu.VMEM((lines, tiles, planes, energies * 4, SUB, LANES), jnp.float32),
            pltpu.VMEM((2, mats, lines, tiles, SUB, LANES), density.dtype),
            pltpu.VMEM((2, tiles, mats, planes, SUB, LANES), density.dtype),
            pltpu.VMEM((total, LANES), jnp.float32),
            pltpu.VMEM((lines, pairs, block, LANES), jnp.float32),
            pltpu.VMEM((lines, pairs, block, LANES), wire),
            pltpu.VMEM((lines, pairs, block, LANES), wire),
            dma((3,)), flag, flag, flag,
            dma((2,)), dma((2,)), dma((2, tiles)), dma((2, tiles)),
            dma((lines, pairs)), dma((lines, pairs)), dma((lines, pairs)), dma((lines, pairs)),
        ],
        compiler_params=pltpu.CompilerParams(collective_id=0, has_side_effects=True),
    )(mixed, color_table, material_weight)
    pixels = pixels.reshape(energies, 4, own // LANES, lines, LANES)
    return pixels.transpose(0, 1, 3, 2, 4).reshape(energies, 4, lines, own)


def solution(mesh):
    return jax.shard_map(
        body,
        mesh=mesh,
        in_specs=(P(None, "depth", "tile", None), P(), P()),
        out_specs=P(None, None, "tile", "depth"),
        check_vma=False,
    )
```

```python
import functools

import jax
import jax.numpy as jnp
from jax import lax
from jax.experimental import pallas as pl
from jax.experimental.pallas import tpu as pltpu
from jax.sharding import PartitionSpec as P

LANES = 128
SUB = 8
LAG = 3
LOG2_E = 1.4426950408889634
PICK = lax.GatherDimensionNumbers(
    offset_dims=(),
    collapsed_slice_dims=(1,),
    start_index_map=(1,),
    operand_batching_dims=(0,),
    start_indices_batching_dims=(0,),
)


def pack_tables(table_ref, tabs):
    for e in range(table_ref.shape[0]):
        word = (
            table_ref[e, 0:1, :]
            + table_ref[e, 1:2, :] * 256
            + table_ref[e, 2:3, :] * 65536
            + lax.shift_left(table_ref[e, 3:4, :], 24)
        )
        bins = word.shape[1]
        pair = (word, pltpu.roll(word, bins - 1, 1))
        for k in range(2):
            for half in range(bins // LANES):
                tabs[e, k, half] = jnp.broadcast_to(
                    pair[k][:, half * LANES : (half + 1) * LANES], (SUB, LANES)
                )


def look_up(tabs, e, k, idx, where_half):
    found = None
    for half in range(tabs.shape[2]):
        piece = lax.gather(
            tabs[e, k, half], idx[:, :, None], PICK, (1, 1),
            mode=lax.GatherScatterMode.PROMISE_IN_BOUNDS,
        )
        found = piece if found is None else jnp.where(where_half == half, piece, found)
    return found


def channels_of(word):
    return (
        (word & 255).astype(jnp.float32),
        (lax.shift_right_logical(word, 8) & 255).astype(jnp.float32),
        (lax.shift_right_logical(word, 16) & 255).astype(jnp.float32),
        lax.shift_right_logical(word, 24).astype(jnp.float32),
    )


def mixer(weight_ref, e):
    w = [weight_ref[e, m] for m in range(weight_ref.shape[1])]

    def mix(values):
        total = w[0] * values[0]
        for m in range(1, len(values)):
            total = total + w[m] * values[m]
        return total

    return mix


def tile_levels(grid_ref, tabs, weight_ref, atten_ref, levels, y, tile, scale):
    mats, planes = grid_ref.shape[:2]
    rows = pl.ds(pl.multiple_of(tile * SUB + SUB, SUB), SUB)
    for z in range(planes):
        mid = [grid_ref[m, z, y, tile].astype(jnp.float32) for m in range(mats)]
        for e in range(weight_ref.shape[0]):
            atten = mixer(weight_ref, e)(mid)
            atten_ref[e, z + 1, y + 1, rows, :] = atten
            level = 255.0 - 255.0 * jnp.exp2((-0.5 * LOG2_E) * atten)
            bin_at = level.astype(jnp.int32)
            frac = level - bin_at.astype(jnp.float32)
            w1 = frac.astype(jnp.bfloat16).astype(jnp.float32)
            w0 = (1.0 - frac).astype(jnp.bfloat16).astype(jnp.float32)
            idx = bin_at & (LANES - 1)
            half = lax.shift_right_logical(bin_at, 7)
            low = channels_of(look_up(tabs, e, 0, idx, half))
            high = channels_of(look_up(tabs, e, 1, idx, half))
            for c in range(4):
                value = w0 * low[c] + w1 * high[c]
                levels[y, tile, z, e * 4 + c] = value * scale if c == 3 else value


def tile_image(atten_ref, levels, y, tile, planes):
    energies = atten_ref.shape[0]
    lane = lax.broadcasted_iota(jnp.int32, (SUB, LANES), 1)
    first, last = lane == 0, lane == LANES - 1
    base = tile * SUB + SUB
    rows = pl.ds(pl.multiple_of(base, SUB), SUB)
    sums, ahead = [], []
    for e in range(energies):
        clear, total = None, [None] * 3
        for z in range(planes):
            here = atten_ref[e, z + 1, y + 1, rows, :]
            dz = atten_ref[e, z + 2, y + 1, rows, :] - atten_ref[e, z, y + 1, rows, :]
            dy = atten_ref[e, z + 1, y + 2, rows, :] - atten_ref[e, z + 1, y, rows, :]
            above = atten_ref[e, z + 1, y + 1, pl.ds(base - 1, SUB), :]
            below = atten_ref[e, z + 1, y + 1, pl.ds(base + 1, SUB), :]
            right = pltpu.roll(jnp.where(first, below, here), LANES - 1, 1)
            left = pltpu.roll(jnp.where(last, above, here), 1, 1)
            dx = right - left
            sq = dz * dz + dy * dy + dx * dx
            inv = lax.rsqrt(sq + 4.0)
            shading = 0.3 + jnp.abs(0.56 * dz + 0.336 * dy + 0.252 * dx) * inv
            opacity = levels[y, tile, z, e * 4 + 3] * (sq * inv * inv)
            lit = opacity * shading
            if z:
                lit = lit * clear
            for c in range(3):
                term = lit * levels[y, tile, z, e * 4 + c]
                total[c] = term if z == 0 else total[c] + term
            transmit = 1.0 - opacity
            clear = transmit if z == 0 else clear * transmit
        sums.append(total)
        ahead.append(clear)
    return sums, ahead


def far_first(mine, step, tiles):
    if tiles & (tiles - 1):
        return (mine + 1 + step) % tiles
    other, result, bit = tiles - 1 - step, 0, 1
    while bit < tiles:
        result = result + bit * ((mine // bit + other // bit) % 2)
        bit *= 2
    return result


WIRE_STEPS = 64000.0
WIRE_ZERO = 32768


def to_wire(value):
    root = jnp.sqrt(jnp.sqrt(jnp.maximum(value, 0.0)))
    return (root * WIRE_STEPS + 0.5).astype(jnp.int32) - WIRE_ZERO


def from_wire(code):
    root = (code.astype(jnp.float32) + float(WIRE_ZERO)) * (1.0 / WIRE_STEPS)
    root = root * root
    return root * root


def render_kernel(
    depth_total, mixed_hbm, table_hbm, weight_hbm, out_ref,
    mixed_ref, table_ref, weight_ref,
    grid_ref, wide, atten_ref, tabs, levels, z_in, y_in, image, pair_in, packed, got,
    in_sem, ready_sem,
    z_send, z_recv, y_send, y_recv, pair_send, pair_recv, send_sem, recv_sem,
):
    mats, planes, lines, tiles = grid_ref.shape[:4]
    strips = tiles * SUB
    energies = weight_ref.shape[0]
    _, pairs, block, _ = got.shape
    count = 2 * pairs
    per_tile = count // tiles
    half_tile = per_tile // 2
    stride = 4 * energies
    pieces = block // stride
    line_rows = strips * stride
    flat = image.reshape(lines * line_rows, LANES)
    me, row = lax.axis_index("depth"), lax.axis_index("tile")
    rows_of = lax.axis_size("tile")
    has_z = (me > 0, me < count - 1)
    has_y = (row > 0, row < rows_of - 1)
    z_peer = (me - 1, me + 1)
    y_peer = (row - 1, row + 1)
    mine = me // per_tile
    core, pair = me % 2, me // 2
    partner = me + 1 - 2 * core
    beside = me + 2 - 4 * (pair % 2)
    layers = pairs // 2
    layer = pair // 2
    first_line = jnp.where(has_y[0], 1, 0)

    def line_of(k):
        return (k + first_line) % lines

    loads = (
        pltpu.make_async_copy(mixed_hbm, mixed_ref, in_sem.at[0]),
        pltpu.make_async_copy(table_hbm, table_ref, in_sem.at[1]),
        pltpu.make_async_copy(weight_hbm, weight_ref, in_sem.at[2]),
    )
    for load in loads:
        load.start()

    barrier = pltpu.get_barrier_semaphore()

    def tell(semaphore, **device):
        pl.semaphore_signal(
            semaphore, inc=1, device_id=device, device_id_type=pl.DeviceIdType.MESH
        )

    tell(barrier, depth=partner)
    tell(barrier, depth=beside)
    others = 2
    outer = me - 1 + 2 * core
    has_outer = jnp.logical_and(outer >= 0, outer < count)

    @pl.when(has_outer)
    def _():
        tell(barrier, depth=outer)
    others = others + jnp.where(has_outer, 1, 0)
    for side in range(2):
        @pl.when(has_y[side])
        def _():
            tell(barrier, tile=y_peer[side])

        others = others + jnp.where(has_y[side], 1, 0)

    @pl.when(layer > 0)
    def _():
        tell(barrier, depth=me - 4)
    others = others + jnp.where(layer < layers - 1, 1, 0) + 2 * layer

    def tell_chips(semaphore):
        def tell_chip(chip, carry):
            tell(semaphore, depth=2 * chip + core)
            return carry

        return tell_chip

    lax.fori_loop(2 * layer + 2, pairs, tell_chips(barrier), 0)

    edge = jnp.zeros((SUB, LANES), jnp.float32)
    blank = jnp.zeros((strips + 2 * SUB, LANES), jnp.float32)

    def clear_edges(z, carry):
        for e in range(energies):
            for y in range(lines):
                atten_ref[e, z + 1, y + 1, 0:SUB, :] = edge
                atten_ref[e, z + 1, y + 1, SUB + strips :, :] = edge
        for side in range(2):
            @pl.when(jnp.logical_not(has_y[side]))
            def _():
                for e in range(energies):
                    atten_ref[e, z + 1, side * (lines + 1)] = blank
        return carry

    lax.fori_loop(0, planes, clear_edges, 0)
    for side in range(2):
        @pl.when(jnp.logical_not(has_z[side]))
        def _():
            for e in range(energies):
                for y in range(lines):
                    atten_ref[e, side * (planes + 1), y + 1] = blank
    loads[0].wait()

    def widen(z, carry):
        for m in range(mats):
            wide[m] = mixed_ref[m, z].astype(jnp.float32)
            for y in range(lines):
                for t in range(tiles):
                    line = wide[m, pl.ds(t * SUB * lines + y, SUB, stride=lines), :]
                    grid_ref[m, z, y, t] = line.astype(grid_ref.dtype)
        return carry

    lax.fori_loop(0, planes, widen, 0)
    pl.semaphore_wait(barrier, others)

    def z_copy(side):
        return pltpu.make_async_remote_copy(
            src_ref=grid_ref.at[:, (planes - 1) * side],
            dst_ref=z_in.at[1 - side],
            send_sem=z_send.at[side],
            recv_sem=z_recv.at[1 - side],
            device_id={"depth": z_peer[side]},
            device_id_type=pl.DeviceIdType.MESH,
        )

    def y_copy(side, t):
        return pltpu.make_async_remote_copy(
            src_ref=grid_ref.at[:, :, (lines - 1) * side, t],
            dst_ref=y_in.at[1 - side, t],
            send_sem=y_send.at[side, t],
            recv_sem=y_recv.at[1 - side, t],
            device_id={"tile": y_peer[side]},
            device_id_type=pl.DeviceIdType.MESH,
        )

    def pair_copy(y, tile):
        return pltpu.make_async_remote_copy(
            src_ref=image.at[y, pl.ds(tile * half_tile, half_tile), 1 - core],
            dst_ref=pair_in.at[y, pl.ds(tile * half_tile, half_tile)],
            send_sem=pair_send.at[y, tile],
            recv_sem=pair_recv.at[y, tile],
            device_id={"depth": partner},
            device_id_type=pl.DeviceIdType.MESH,
        )

    def block_copy(y, chip, source):
        return pltpu.make_async_remote_copy(
            src_ref=packed.at[y, chip],
            dst_ref=got.at[y, source],
            send_sem=send_sem.at[y, chip],
            recv_sem=recv_sem.at[y, source],
            device_id={"depth": 2 * chip + core},
            device_id_type=pl.DeviceIdType.MESH,
        )

    upper = lax.broadcasted_iota(jnp.int32, (SUB, LANES), 0) < energies

    def both_halves(value):
        return jnp.where(upper, pltpu.roll(value, energies, 0), value)

    def forward(k):
        y, tile = line_of(k // tiles), far_first(mine, k % tiles, tiles)
        pair_copy(y, tile).wait_recv()
        for h in range(half_tile):
            chip = tile * half_tile + h
            for s in range(pieces):
                front, back = [], []
                for v in range(2):
                    at = s * stride + v * SUB
                    ours = image[y, chip, core, at : at + SUB, :]
                    theirs = pair_in[y, chip, at : at + SUB, :]
                    front.append(jnp.where(core == 0, ours, theirs))
                    back.append(jnp.where(core == 0, theirs, ours))
                clear = both_halves(front[1])
                low = front[0] + clear * back[0]
                high = jnp.where(upper, front[1], 0.0) + clear * back[1]
                high = jnp.where(upper, high, 1.0 - high)
                packed[y, chip, s * stride : (s + 1) * stride, :] = to_wire(
                    jnp.concatenate([low, high], axis=0)
                ).astype(packed.dtype)

            @pl.when(chip != pair)
            def _():
                block_copy(y, chip, pair).start()

    lax.fori_loop(0, 2 * layer, tell_chips(ready_sem), 0)
    for side in range(2):
        @pl.when(has_z[side])
        def _():
            z_copy(side).start()
    for i in range(tiles):
        for side in range(2):
            @pl.when(has_y[side])
            def _():
                y_copy(side, far_first(mine, i, tiles)).start()

    loads[1].wait()
    loads[2].wait()
    pack_tables(table_ref, tabs)
    steps = tiles * lines
    lag = jnp.minimum(3 + (layers - 1 - layer) // 2, steps - 1)

    def level_step(j, carry):
        tile_levels(
            grid_ref, tabs, weight_ref, atten_ref, levels, line_of(j // tiles), j % tiles,
            6.0 / depth_total / 255.0,
        )
        return carry

    lax.fori_loop(0, steps, level_step, 0)

    for side in range(2):
        @pl.when(has_z[side])
        def _():
            z_copy(1 - side).wait_recv()
            for t in range(tiles):
                for y in range(lines):
                    mid = [z_in[side, m, y, t].astype(jnp.float32) for m in range(mats)]
                    for e in range(energies):
                        atten_ref[
                            e, side * (planes + 1), y + 1, SUB + t * SUB : 2 * SUB + t * SUB, :
                        ] = mixer(weight_ref, e)(mid)

    def image_step(k, carry):
        @pl.when(jnp.logical_and(k == lag, layer < layers - 1))
        def _():
            pl.semaphore_wait(ready_sem, 2 * (layers - 1 - layer))

        @pl.when(k >= lag)
        def _():
            forward(k - lag)

        y, tile = line_of(k // tiles), far_first(mine, k % tiles, tiles)
        here = pl.ds(pl.multiple_of(tile * SUB + SUB, SUB), SUB)
        for side in range(2):
            @pl.when(jnp.logical_and(has_y[side], y == side * (lines - 1)))
            def _():
                y_copy(1 - side, tile).wait_recv()
                for z in range(planes):
                    mid = [y_in[side, tile, m, z].astype(jnp.float32) for m in range(mats)]
                    for e in range(energies):
                        atten_ref[e, z + 1, side * (lines + 1), here, :] = mixer(weight_ref, e)(mid)

        sums, ahead = tile_image(atten_ref, levels, y, tile, planes)
        for e in range(energies):
            for c in range(4):
                value = sums[e][c] * (1.0 / 255.0) if c < 3 else ahead[e]
                start = y * line_rows + tile * (SUB * stride) + c * energies + e
                flat[pl.ds(start, SUB, stride=stride), :] = value
        pair_copy(y, tile).start()

        return carry

    lax.fori_loop(0, steps, image_step, 0)

    def late_step(k, carry):
        forward(k)
        return carry

    lax.fori_loop(steps - lag, steps, late_step, 0)
    for y in range(lines):
        got[y, pair] = packed[y, pair]

    for k in range(lines):
        y = line_of(k)
        low, high, clear = [None] * pieces, [None] * pieces, [None] * pieces
        for n in range(pairs):
            @pl.when(pair != n)
            def _():
                block_copy(y, n, n).wait_recv()
            for s in range(pieces):
                both = from_wire(
                    got[y, n, s * stride : (s + 1) * stride, :].astype(jnp.int32)
                )
                a, b = both[0:SUB], both[SUB:]
                seen = both_halves(1.0 - b)
                low[s] = a if n == 0 else low[s] + clear[s] * a
                high[s] = b if n == 0 else high[s] + clear[s] * b
                clear[s] = seen if n == 0 else clear[s] * seen
        for s in range(pieces):
            parts = (low[s], jnp.where(upper, high[s], 1.0 - clear[s]))
            for c in range(4):
                value = parts[c // 2][(c % 2) * energies : (c % 2 + 1) * energies]
                out_ref[
                    pl.ds((c * pieces + s) * lines + y, energies, stride=4 * pieces * lines), :
                ] = value

    for side in range(2):
        @pl.when(has_z[side])
        def _():
            z_copy(side).wait_send()
        @pl.when(has_y[side])
        def _():
            for t in range(tiles):
                y_copy(side, t).wait_send()
    for y in range(lines):
        for t in range(tiles):
            pair_copy(y, t).wait_send()
        for n in range(pairs):
            @pl.when(pair != n)
            def _():
                block_copy(y, n, n).wait_send()


def body(density, material_weight, color_table):
    mats, planes, lines, columns = density.shape
    energies = material_weight.shape[0]
    count = lax.axis_size("depth")
    strips = columns // LANES
    tiles = strips // SUB
    mixed = density.reshape(mats, planes, lines, strips, LANES).transpose(0, 1, 3, 2, 4)
    mixed = mixed.reshape(mats, planes, strips * lines, LANES)
    hbm = pl.BlockSpec(memory_space=pl.ANY)
    total = strips * 4 * energies * lines
    own = columns // count
    block = total // count // lines
    pairs = count // 2
    dma = pltpu.SemaphoreType.DMA
    flag = pltpu.SemaphoreType.REGULAR
    wire = jnp.int16
    pixels = pl.pallas_call(
        functools.partial(render_kernel, planes * count),
        out_shape=pltpu.VMEM((total // count, LANES), jnp.float32),
        in_specs=[hbm, hbm, hbm],
        out_specs=pl.BlockSpec(memory_space=pltpu.VMEM),
        scratch_shapes=[
            pltpu.VMEM(mixed.shape, density.dtype),
            pltpu.VMEM(color_table.shape, color_table.dtype),
            pltpu.SMEM(material_weight.shape, material_weight.dtype),
            pltpu.VMEM((mats, planes, lines, tiles, SUB, LANES), density.dtype),
            pltpu.VMEM((mats, strips * lines, LANES), jnp.float32),
            pltpu.VMEM((energies, planes + 2, lines + 2, strips + 2 * SUB, LANES), jnp.float32),
            pltpu.VMEM((energies, 2, color_table.shape[2] // LANES, SUB, LANES), jnp.int32),
            pltpu.VMEM((lines, tiles, planes, energies * 4, SUB, LANES), jnp.float32),
            pltpu.VMEM((2, mats, lines, tiles, SUB, LANES), density.dtype),
            pltpu.VMEM((2, tiles, mats, planes, SUB, LANES), density.dtype),
            pltpu.VMEM((lines, pairs, 2, block, LANES), jnp.float32),
            pltpu.VMEM((lines, pairs, block, LANES), jnp.float32),
            pltpu.VMEM((lines, pairs, block, LANES), wire),
            pltpu.VMEM((lines, pairs, block, LANES), wire),
            dma((3,)), flag,
            dma((2,)), dma((2,)), dma((2, tiles)), dma((2, tiles)),
            dma((lines, tiles)), dma((lines, tiles)), dma((lines, pairs)), dma((lines, pairs)),
        ],
        compiler_params=pltpu.CompilerParams(collective_id=0, has_side_effects=True),
    )(mixed, color_table, material_weight)
    pixels = pixels.reshape(energies, 4, own // LANES, lines, LANES)
    return pixels.transpose(0, 1, 3, 2, 4).reshape(energies, 4, lines, own)


def solution(mesh):
    return jax.shard_map(
        body,
        mesh=mesh,
        in_specs=(P(None, "depth", "tile", None), P(), P()),
        out_specs=P(None, None, "tile", "depth"),
        check_vma=False,
    )
```
